32 devices in a mesh: wide: 8 (over z, x), narrow: 4 (over y, core).
Axes of the slice: x: 2, y: 2, z: 4, core: 2. Of those that a mesh axis runs over, the one named last changes fastest.
Arguments:
- points: bfloat16 [32768, 256], P('wide'), may hold values from -6 to 6
- q_init: float32 [16, 32768], P(None, 'wide'), may hold values from -80 to 80
- pairs: int32 [2, 2048], P(None, ('wide', 'narrow')), may hold values from 0 to 255, as said below
Outputs:
- basis: float32 [16, 32768], P(None, 'wide')
- coeffs: float32 [3, 2, 16, 16], replicated
The draws below stay inside these ranges and needn't reach their ends.
Inputs may be any that keep to these rules, and one draw needn't show every extreme that they name: `pairs`: pair number g * 4 * 64 + m * 64 + o * 8 + c (g < 8, m < 4, o < 8, c < 8) has its first block in g * 32 .. (g + 1) * 32 - 1 and its second block in o * 32 .. (o + 1) * 32 - 1; the two ends of a pair differ.
All inputs are finite; a program needn't handle non-finite values.
Results may differ from the reference program's by a relative error of at most 0.0015.
Values may be sent and summed in bfloat16 or wider, within the bound.
A program may use at most 64 MiB of HBM per device.

```python
import jax
import jax.numpy as jnp
from jax import lax

F = 256
R = 16
BS = 128
STEPS = 3
PAIRS_DEV = 64
BLOCKS_PER_SHARD = 32
CAP = 8
NB = 256
NPTS = 32768
TOTAL_PAIRS = 2048
N_NARROW = 4


def draw_pairs(key, part):
    slot = jnp.arange(TOTAL_PAIRS, dtype=jnp.int32)
    device = slot // PAIRS_DEV
    group = device // N_NARROW
    owner = slot % PAIRS_DEV // CAP
    first_row = jax.random.randint(jax.random.fold_in(key, 11), (TOTAL_PAIRS,), 0, BLOCKS_PER_SHARD, dtype=jnp.int32)
    offset = jax.random.randint(jax.random.fold_in(key, 12), (TOTAL_PAIRS,), 1, BLOCKS_PER_SHARD, dtype=jnp.int32)
    other = jax.random.randint(jax.random.fold_in(key, 13), (TOTAL_PAIRS,), 0, BLOCKS_PER_SHARD, dtype=jnp.int32)
    second_row = jnp.where(owner == group, (first_row + offset) % BLOCKS_PER_SHARD, other)
    first_id = group * BLOCKS_PER_SHARD + first_row
    second_id = owner * BLOCKS_PER_SHARD + second_row
    return jnp.stack([first_id, second_id]).astype(jnp.int32)


def draw_q_init(key, part):
    noise = jax.random.normal(jax.random.fold_in(key, 21), (R, NPTS), jnp.float32)
    noise = jnp.clip(noise, -6.0, 6.0)
    scales = jnp.exp(jax.random.uniform(jax.random.fold_in(key, 22), (1, NPTS), jnp.float32, 0.0, 2.3))
    values = scales * noise
    return jnp.clip(values, -80.0, 80.0).astype(jnp.float32)


def level_of(stream_key, extent, cuts, low, largest):
    loudness = 1.0
    for position, shards_of in cuts:
        steps = jax.random.uniform(jax.random.fold_in(jax.random.fold_in(stream_key, 6), position), (shards_of,), jnp.float32, low / len(cuts), largest / len(cuts))
        loudness = loudness * jnp.repeat(jnp.exp(steps), extent[position] // shards_of).reshape((-1,) + (1,) * (len(extent) - 1 - position))
    return loudness


def centred(rng, extent, deviation, limit, cuts=(), kind=jnp.bfloat16):
    entries = deviation * jax.random.normal(rng, extent, jnp.float32)
    if cuts:
        entries = entries * level_of(rng, extent, cuts, -0.22, 0.18)
    return jnp.clip(entries, -limit, limit).astype(kind)


def setup_inputs(seed: int = 0) -> dict:
    keys = jax.random.split(jax.random.key(seed), 4)
    points = centred(keys[0], (NPTS, F), 1.0, 6.0, ((0, 8),))
    q_init = draw_q_init(jax.random.fold_in(keys[3], 71), 0)
    pairs = draw_pairs(jax.random.fold_in(keys[3], 71), 0)
    return {"points": points, "q_init": q_init, "pairs": pairs}


KERNEL_FACTOR = 3.0
EPSILON = 1e-06
HIGH = lax.Precision.HIGHEST

def unit_rows(points):
    wide32 = points.astype(jnp.float32)
    scaled = wide32 * lax.rsqrt(lax.optimization_barrier(jnp.sum(wide32 * wide32, axis=-1, keepdims=True)) + EPSILON)
    return scaled.astype(jnp.bfloat16)

def apply_kernel(unit, vectors, pairs):
    rows = vectors.reshape(R, NB, BS).transpose(1, 0, 2)
    point_groups = pairs.reshape(2, TOTAL_PAIRS // PAIRS_DEV, PAIRS_DEV).transpose(1, 0, 2)

    def single_group(total, ends):
        first = ends[0]
        second = ends[1]
        inner_products = jnp.einsum('paf,pbf->pab', unit[first].astype(jnp.float32), unit[second].astype(jnp.float32), precision=HIGH)
        kernel_values = jnp.exp(KERNEL_FACTOR * (inner_products - 1.0))
        to_first = jnp.einsum('pab,prb->pra', kernel_values, rows[second], precision=HIGH)
        to_second = jnp.einsum('pab,pra->prb', kernel_values, rows[first], precision=HIGH)
        return (total.at[first].add(to_first).at[second].add(to_second), None)
    total = lax.scan(single_group, jnp.zeros_like(rows), point_groups)[0]
    return total.transpose(1, 0, 2).reshape(R, NPTS)

def reference(points, q_init, pairs):
    unit = unit_rows(points).reshape(NB, BS, F)
    gram0 = jnp.dot(q_init, q_init.T, precision=HIGH) / NPTS
    factor0 = jnp.linalg.cholesky(gram0)
    current = lax.linalg.triangular_solve(factor0, q_init, left_side=True, lower=True)
    previous = jnp.zeros_like(current)
    last = jnp.zeros((R, R), jnp.float32).astype(current.dtype)
    records = []
    for step in range(STEPS):
        image = apply_kernel(unit, current, pairs)
        residual = image - jnp.dot(last.T, previous, precision=HIGH)
        along = jnp.dot(current, residual.T, precision=HIGH) / NPTS
        remainder = residual - jnp.dot(along.T, current, precision=HIGH)
        gram = jnp.dot(remainder, remainder.T, precision=HIGH) / NPTS
        factor = jnp.linalg.cholesky(gram)
        records.append(jnp.stack([along, factor]))
        previous = current
        last = factor
        current = lax.linalg.triangular_solve(factor, remainder, left_side=True, lower=True)
    return (current, jnp.stack(records))
```

```python
import functools

import jax
import jax.numpy as jnp
from jax import lax
from jax.experimental import pallas as pl
from jax.experimental.pallas import tpu as pltpu
from jax.sharding import PartitionSpec as P

BS = 128
STEPS = 3
KERNEL_FACTOR = 3.0
EPSILON = 1e-06
HIGH = lax.Precision.HIGHEST
MESH = pl.DeviceIdType.MESH


def unit_rows(points):
    wide32 = points.astype(jnp.float32)
    scaled = wide32 * lax.rsqrt(jnp.sum(wide32 * wide32, axis=-1, keepdims=True) + EPSILON)
    return scaled.astype(jnp.bfloat16)


def split(x):
    high = x.astype(jnp.bfloat16)
    return high, (x - high.astype(jnp.float32)).astype(jnp.bfloat16)


def dot32(a, b):
    return jnp.dot(a, b, precision=HIGH, preferred_element_type=jnp.float32)


def dot_nt(a, b, precision=None):
    return lax.dot_general(
        a, b, (((1,), (1,)), ((), ())), precision=precision, preferred_element_type=jnp.float32
    )


def tiles_kernel(capacity, me_ref, first_ref, unit_ref, second_ref, out_ref):
    d = pl.program_id(0)
    for c in range(capacity):
        s = dot_nt(unit_ref[first_ref[d * capacity + c]], second_ref[0, c])
        high, low = split(jnp.exp(KERNEL_FACTOR * (s - 1.0)))
        out_ref[c, :, :BS] = high
        out_ref[c, :, BS:] = low


def make_tiles(me, first, unit, second):
    wide_count, capacity, _, width = second.shape
    own_blocks = unit.shape[0]
    spec = pltpu.PrefetchScalarGridSpec(
        num_scalar_prefetch=2,
        grid=(wide_count,),
        in_specs=[
            pl.BlockSpec((own_blocks, BS, width), lambda d, m, f: (0, 0, 0)),
            pl.BlockSpec(
                (1, capacity, BS, width),
                lambda d, m, f: (lax.rem(m[0] - d + wide_count, wide_count), 0, 0, 0),
            ),
        ],
        out_specs=pl.BlockSpec((capacity, BS, 2 * BS), lambda d, m, f: (d, 0, 0)),
    )
    return pl.pallas_call(
        functools.partial(tiles_kernel, capacity),
        grid_spec=spec,
        out_shape=jax.ShapeDtypeStruct((wide_count * capacity, BS, 2 * BS), jnp.bfloat16),
        name="tiles",
    )(me, first, unit, second)


def factor_of(gram, r):
    i = lax.broadcasted_iota(jnp.int32, (r, r), 0)
    j = lax.broadcasted_iota(jnp.int32, (r, r), 1)
    both_i = lax.broadcasted_iota(jnp.int32, (r, 2 * r), 0)
    m = jnp.concatenate([gram, (i == j).astype(jnp.float32)], axis=1)
    lower = jnp.zeros((r, r), jnp.float32)
    for k in range(r):
        inv = 1.0 / jnp.sqrt(m[k : k + 1, k : k + 1])
        row = m[k : k + 1, :] * inv
        col = m[:, k : k + 1] * inv
        lower = jnp.where((j == k) & (i >= k), col, lower)
        m = jnp.where(both_i == k, row, jnp.where(both_i > k, m - col * row, m))
    upper = jnp.where(j >= i, m[:, :r], 0.0)
    inverse = jnp.where(j <= i, m[:, r:], 0.0)
    return lower, upper, inverse


def main_kernel(
    dims, first, local, owners, tiles, q_ref, out, coef,
    sb, rb, sb2, rb2, tf, pb, rs, ag, xs, blocks, prev, up, gs, gr,
    s1, r1, s2, r2, s3, r3, s4, r4, s5, r5,
):
    W, N, C, R, B, total = dims
    CR = C * R
    RN = R // N
    PR = RN * B
    me = lax.axis_index("wide")
    nar = lax.axis_index("narrow")

    def up_peer(d):
        return lax.rem(me + d, W)

    def down_peer(d):
        return lax.rem(me - d + W, W)

    barrier = pltpu.get_barrier_semaphore()
    for d in range(1, W):
        pl.semaphore_signal(barrier, inc=1, device_id={"wide": up_peer(d)}, device_id_type=MESH)
    for d in range(1, N):
        pl.semaphore_signal(
            barrier, inc=1, device_id={"narrow": lax.rem(nar + d, N)}, device_id_type=MESH
        )
    pl.semaphore_wait(barrier, W - 1 + N - 1)

    def request(d):
        rows = pl.ds(d * CR, CR)
        return pltpu.make_async_remote_copy(
            src_ref=sb.at[rows], dst_ref=rb.at[rows], send_sem=s1.at[d], recv_sem=r1.at[d],
            device_id={"wide": up_peer(d)}, device_id_type=MESH,
        )

    def answer(d):
        rows = pl.ds(d * CR, CR)
        return pltpu.make_async_remote_copy(
            src_ref=sb2.at[rows], dst_ref=rb2.at[rows], send_sem=s2.at[d], recv_sem=r2.at[d],
            device_id={"wide": down_peer(d)}, device_id_type=MESH,
        )

    def scatter(d):
        return pltpu.make_async_remote_copy(
            src_ref=pb.at[pl.ds(lax.rem(nar + d, N) * PR, PR)], dst_ref=rs.at[d],
            send_sem=s3.at[d], recv_sem=r3.at[d],
            device_id={"narrow": lax.rem(nar + d, N)}, device_id_type=MESH,
        )

    def gather(d):
        mine = pl.ds(nar * PR, PR)
        return pltpu.make_async_remote_copy(
            src_ref=rs.at[0], dst_ref=ag.at[mine], send_sem=s4.at[d], recv_sem=r4.at[d],
            device_id={"narrow": lax.rem(nar + d, N)}, device_id_type=MESH,
        )

    def gathered(d):
        theirs = pl.ds(lax.rem(nar - d + N, N) * PR, PR)
        return pltpu.make_async_remote_copy(
            src_ref=rs.at[0], dst_ref=ag.at[theirs], send_sem=s4.at[d], recv_sem=r4.at[d],
            device_id={"narrow": lax.rem(nar + d, N)}, device_id_type=MESH,
        )

    def gram_copy(d):
        return pltpu.make_async_remote_copy(
            src_ref=gs, dst_ref=gr.at[d], send_sem=s5.at[d], recv_sem=r5.at[d],
            device_id={"wide": up_peer(d)}, device_id_type=MESH,
        )

    def gram_sum(value):
        gs[:, : 2 * R] = value
        gr[0, :, : 2 * R] = value
        for d in range(1, W):
            gram_copy(d).start()
        for d in range(1, W):
            gram_copy(d).wait_recv()
        summed = jnp.zeros((2 * R, 2 * R), jnp.float32)
        for s in range(W):
            summed += gr[lax.rem(me - s + W, W)][:, : 2 * R]
        for d in range(1, W):
            gram_copy(d).wait_send()
        return summed / total

    gs[...] = jnp.zeros_like(gs)
    xs[:R, :] = q_ref[...]
    xs[R:, :] = jnp.zeros((R, B * BS), jnp.float32)
    prev[...] = jnp.zeros_like(prev)
    up[...] = jnp.zeros_like(up)
    start = gram_sum(dot_nt(xs[...], xs[...], HIGH))
    _, _, inverse0 = factor_of(start[:R, :R], R)
    xs[:R, :] = dot32(inverse0, q_ref[...])

    def step(k, carry):
        for b in range(B):
            blocks[b] = xs[:R, b * BS : (b + 1) * BS]
        for d in range(W):
            for c in range(C):
                value = blocks[local[d * C + c]]
                (rb if d == 0 else sb)[pl.ds((d * C + c) * R, R), :] = value
            if d:
                request(d).start()

        def group(d, carry):
            @pl.when(d > 0)
            def _():
                request(d).wait_recv()

            for c in range(C):
                p = d * C + c
                rows = pl.ds(pl.multiple_of(p * R, R), R)
                tile = tiles[p]
                high, low = split(rb[rows, :])
                left = jnp.concatenate(
                    [
                        jnp.concatenate([high, high], axis=1),
                        jnp.concatenate([low, jnp.zeros_like(low)], axis=1),
                    ],
                    axis=0,
                )
                both = dot_nt(left, tile)
                tf[rows, :] = both[:R] + both[R:]
                high, low = split(blocks[first[p]])
                both = jnp.dot(
                    jnp.concatenate([high, low], axis=0), tile, preferred_element_type=jnp.float32
                )
                sb2[rows, :] = both[:R, :BS] + both[R:, :BS] + both[:R, BS:]

            @pl.when(d > 0)
            def _():
                answer(d).start()

            return carry

        lax.fori_loop(0, W, group, 0)
        rb2[pl.ds(0, CR), :] = sb2[pl.ds(0, CR), :]
        for d in range(1, W):
            answer(d).wait_recv()

        one_hot = owners[...]
        for n in range(1, N + 1):
            part = lax.rem(nar + n, N)
            for q in range(RN):
                r = part * RN + q
                x = jnp.concatenate(
                    [tf[pl.ds(r, W * C, stride=R), :], rb2[pl.ds(r, W * C, stride=R), :]], axis=0
                )
                high, low = split(x)
                value = jnp.dot(
                    one_hot,
                    jnp.concatenate([high, low], axis=0),
                    preferred_element_type=jnp.float32,
                )
                if n == N:
                    rs[0, pl.ds(q * B, B), :] = value
                else:
                    pb[pl.ds(pl.multiple_of(part * PR + q * B, B), B), :] = value
            if n < N:
                scatter(n).start()
        for d in range(1, N):
            scatter(d).wait_recv()
        mine = rs[0]
        for d in range(1, N):
            mine += rs[d]
        rs[0] = mine
        for d in range(1, N):
            gather(d).start()
        ag[pl.ds(pl.multiple_of(nar * PR, PR), PR), :] = mine
        for d in range(1, N):
            gathered(d).wait_recv()

        for b in range(B):
            xs[R:, b * BS : (b + 1) * BS] = ag[pl.ds(b, R, stride=B), :]
        xs[R:, :] = xs[R:, :] - dot32(up[...], prev[...])
        summed = gram_sum(dot_nt(xs[...], xs[...], HIGH))
        basis_gram = summed[:R, :R]
        along = summed[:R, R:]
        along_t = summed[R:, :R]
        raw = summed[R:, R:]
        gram = raw - 2.0 * dot32(along_t, along) + dot32(along_t, dot32(basis_gram, along))
        lower, upper, inverse = factor_of(gram, R)
        coef[k, 0] = along
        coef[k, 1] = lower
        prev[...] = xs[:R, :]
        up[...] = upper
        mix = jnp.concatenate([-dot32(inverse, along_t), inverse], axis=1)
        xs[:R, :] = dot32(mix, xs[...])

        for d in range(1, W):
            request(d).wait_send()
            answer(d).wait_send()
        for d in range(1, N):
            scatter(d).wait_send()
            gather(d).wait_send()
        return carry

    lax.fori_loop(0, STEPS, step, 0)
    out[...] = xs[:R, :]


def lanczos(first, local, owners, tiles, q_init, wide_count, narrow_count, total):
    R, cols = q_init.shape
    B = cols // BS
    pair_count = first.shape[0]
    C = pair_count // wide_count
    dims = (wide_count, narrow_count, C, R, B, total)
    vmem = pl.BlockSpec(memory_space=pltpu.VMEM)
    smem = pl.BlockSpec(memory_space=pltpu.SMEM)
    f32 = jnp.float32
    pairs_buf = pltpu.VMEM((pair_count * R, BS), f32)
    part = R // narrow_count * B
    wide_sem = pltpu.SemaphoreType.DMA((wide_count,))
    narrow_sem = pltpu.SemaphoreType.DMA((narrow_count,))
    return pl.pallas_call(
        functools.partial(main_kernel, dims),
        out_shape=(
            jax.ShapeDtypeStruct((R, cols), f32),
            jax.ShapeDtypeStruct((STEPS, 2, R, R), f32),
        ),
        in_specs=[smem, smem, vmem, vmem, vmem],
        out_specs=(vmem, vmem),
        scratch_shapes=[
            pairs_buf, pairs_buf, pairs_buf, pairs_buf, pairs_buf,
            pltpu.VMEM((R * B, BS), f32),
            pltpu.VMEM((narrow_count, part, BS), f32),
            pltpu.VMEM((R * B, BS), f32),
            pltpu.VMEM((2 * R, cols), f32),
            pltpu.VMEM((B, R, BS), f32),
            pltpu.VMEM((R, cols), f32),
            pltpu.VMEM((R, R), f32),
            pltpu.VMEM((2 * R, BS), f32),
            pltpu.VMEM((wide_count, 2 * R, BS), f32),
            wide_sem, wide_sem, wide_sem, wide_sem,
            narrow_sem, narrow_sem, narrow_sem, narrow_sem,
            wide_sem, wide_sem,
        ],
        compiler_params=pltpu.CompilerParams(collective_id=0, has_side_effects=True),
        name="lanczos",
    )(first, local, owners, tiles, q_init)


def per_device(points, q_init, pairs):
    wide_count = lax.axis_size("wide")
    narrow_count = lax.axis_size("narrow")
    me = lax.axis_index("wide")
    own_blocks = points.shape[0] // BS
    width = points.shape[1]
    pair_count = pairs.shape[1]
    capacity = pair_count // wide_count
    total = own_blocks * BS * wide_count
    unit = unit_rows(points).reshape(own_blocks, BS, width)
    wanted = pairs[1].reshape(wide_count, capacity)
    local_ids = (
        lax.all_to_all(wanted, "wide", split_axis=0, concat_axis=0, tiled=True) - me * own_blocks
    )
    second = lax.all_to_all(unit[local_ids], "wide", split_axis=0, concat_axis=0, tiled=True)
    turn = jnp.arange(wide_count, dtype=jnp.int32)
    first_rows = (pairs[0] - me * own_blocks).reshape(wide_count, capacity)
    first = first_rows[(me - turn) % wide_count].reshape(pair_count)
    local = local_ids.reshape(wide_count, capacity)[(me + turn) % wide_count].reshape(pair_count)
    targets = jnp.concatenate([first, local, first, local])
    owners = (jnp.arange(own_blocks, dtype=jnp.int32)[:, None] == targets[None, :]).astype(
        jnp.bfloat16
    )
    tiles = make_tiles(jnp.reshape(me, (1,)).astype(jnp.int32), first, unit, second.reshape(wide_count, capacity, BS, width))
    return lanczos(first, local, owners, tiles, q_init, wide_count, narrow_count, total)


def solution(mesh):
    placed = (P("wide", None), P(None, "wide"), P(None, ("wide", "narrow")))
    return jax.shard_map(
        per_device, mesh=mesh, in_specs=placed, out_specs=(P(None, "wide"), P()), check_vma=False
    )
```

```python
import functools

import jax
import jax.numpy as jnp
from jax import lax
from jax.experimental import pallas as pl
from jax.experimental.pallas import tpu as pltpu
from jax.sharding import PartitionSpec as P

BS = 128
STEPS = 3
KERNEL_FACTOR = 3.0
EPSILON = 1e-06
HIGH = lax.Precision.HIGHEST
MESH = pl.DeviceIdType.MESH


def unit_rows(points):
    wide32 = points.astype(jnp.float32)
    scaled = wide32 * lax.rsqrt(jnp.sum(wide32 * wide32, axis=-1, keepdims=True) + EPSILON)
    return scaled.astype(jnp.bfloat16)


def split(x):
    high = x.astype(jnp.bfloat16)
    return high, (x - high.astype(jnp.float32)).astype(jnp.bfloat16)


def dot32(a, b):
    return jnp.dot(a, b, precision=HIGH, preferred_element_type=jnp.float32)


def dot_nt(a, b, precision=None):
    return lax.dot_general(
        a, b, (((1,), (1,)), ((), ())), precision=precision, preferred_element_type=jnp.float32
    )


def tiles_kernel(capacity, me_ref, first_ref, unit_ref, second_ref, out_ref):
    d = pl.program_id(0)
    for c in range(capacity):
        s = dot_nt(unit_ref[first_ref[d * capacity + c]], second_ref[0, c])
        high, low = split(jnp.exp(KERNEL_FACTOR * (s - 1.0)))
        out_ref[c, :, :BS] = high
        out_ref[c, :, BS:] = low


def make_tiles(me, first, unit, second):
    wide_count, capacity, _, width = second.shape
    own_blocks = unit.shape[0]
    spec = pltpu.PrefetchScalarGridSpec(
        num_scalar_prefetch=2,
        grid=(wide_count,),
        in_specs=[
            pl.BlockSpec((own_blocks, BS, width), lambda d, m, f: (0, 0, 0)),
            pl.BlockSpec(
                (1, capacity, BS, width),
                lambda d, m, f: (lax.rem(m[0] - d + wide_count, wide_count), 0, 0, 0),
            ),
        ],
        out_specs=pl.BlockSpec((capacity, BS, 2 * BS), lambda d, m, f: (d, 0, 0)),
    )
    return pl.pallas_call(
        functools.partial(tiles_kernel, capacity),
        grid_spec=spec,
        out_shape=jax.ShapeDtypeStruct((wide_count * capacity, BS, 2 * BS), jnp.bfloat16),
        name="tiles",
    )(me, first, unit, second)


def factor_of(gram, r):
    i = lax.broadcasted_iota(jnp.int32, (r, r), 0)
    j = lax.broadcasted_iota(jnp.int32, (r, r), 1)
    both_i = lax.broadcasted_iota(jnp.int32, (r, 2 * r), 0)
    m = jnp.concatenate([gram, (i == j).astype(jnp.float32)], axis=1)
    lower = jnp.zeros((r, r), jnp.float32)
    for k in range(r):
        inv = 1.0 / jnp.sqrt(m[k : k + 1, k : k + 1])
        row = m[k : k + 1, :] * inv
        col = m[:, k : k + 1] * inv
        lower = jnp.where((j == k) & (i >= k), col, lower)
        m = jnp.where(both_i == k, row, jnp.where(both_i > k, m - col * row, m))
    upper = jnp.where(j >= i, m[:, :r], 0.0)
    inverse = jnp.where(j <= i, m[:, r:], 0.0)
    return lower, upper, inverse


def main_kernel(
    dims, first, local, owners, tiles, q_ref, out, coef,
    sb, rb, sb2, rb2, tf, pb, rs, ag, xs, blocks, prev, up, gs, gr,
    s1, r1, s2, r2, s3, r3, s4, r4, s5, r5,
):
    W, N, C, R, B, total = dims
    CR = C * R
    RN = R // N
    PR = RN * B
    me = lax.axis_index("wide")
    nar = lax.axis_index("narrow")

    def up_peer(d):
        return lax.rem(me + d, W)

    def down_peer(d):
        return lax.rem(me - d + W, W)

    barrier = pltpu.get_barrier_semaphore()
    for d in range(1, W):
        pl.semaphore_signal(barrier, inc=1, device_id={"wide": up_peer(d)}, device_id_type=MESH)
    for d in range(1, N):
        pl.semaphore_signal(
            barrier, inc=1, device_id={"narrow": lax.rem(nar + d, N)}, device_id_type=MESH
        )
    pl.semaphore_wait(barrier, W - 1 + N - 1)

    def request(d):
        rows = pl.ds(d * CR, CR)
        return pltpu.make_async_remote_copy(
            src_ref=sb.at[rows], dst_ref=rb.at[rows], send_sem=s1.at[d], recv_sem=r1.at[d],
            device_id={"wide": up_peer(d)}, device_id_type=MESH,
        )

    def answer(d):
        rows = pl.ds(d * CR, CR)
        return pltpu.make_async_remote_copy(
            src_ref=sb2.at[rows], dst_ref=rb2.at[rows], send_sem=s2.at[d], recv_sem=r2.at[d],
            device_id={"wide": down_peer(d)}, device_id_type=MESH,
        )

    def scatter(d):
        return pltpu.make_async_remote_copy(
            src_ref=pb.at[pl.ds(lax.rem(nar + d, N) * PR, PR)], dst_ref=rs.at[d],
            send_sem=s3.at[d], recv_sem=r3.at[d],
            device_id={"narrow": lax.rem(nar + d, N)}, device_id_type=MESH,
        )

    def gather(d):
        mine = pl.ds(nar * PR, PR)
        return pltpu.make_async_remote_copy(
            src_ref=rs.at[0], dst_ref=ag.at[mine], send_sem=s4.at[d], recv_sem=r4.at[d],
            device_id={"narrow": lax.rem(nar + d, N)}, device_id_type=MESH,
        )

    def gathered(d):
        theirs = pl.ds(lax.rem(nar - d + N, N) * PR, PR)
        return pltpu.make_async_remote_copy(
            src_ref=rs.at[0], dst_ref=ag.at[theirs], send_sem=s4.at[d], recv_sem=r4.at[d],
            device_id={"narrow": lax.rem(nar + d, N)}, device_id_type=MESH,
        )

    def gram_copy(d):
        return pltpu.make_async_remote_copy(
            src_ref=gs, dst_ref=gr.at[d], send_sem=s5.at[d], recv_sem=r5.at[d],
            device_id={"wide": up_peer(d)}, device_id_type=MESH,
        )

    def gram_sum(value):
        gs[:, : 2 * R] = value
        gr[0, :, : 2 * R] = value
        for d in range(1, W):
            gram_copy(d).start()
        for d in range(1, W):
            gram_copy(d).wait_recv()
        summed = jnp.zeros((2 * R, 2 * R), jnp.float32)
        for s in range(W):
            summed += gr[lax.rem(me - s + W, W)][:, : 2 * R]
        for d in range(1, W):
            gram_copy(d).wait_send()
        return summed / total

    gs[...] = jnp.zeros_like(gs)
    xs[:R, :] = q_ref[...]
    xs[R:, :] = jnp.zeros((R, B * BS), jnp.float32)
    prev[...] = jnp.zeros_like(prev)
    up[...] = jnp.zeros_like(up)
    start = gram_sum(dot_nt(xs[...], xs[...], HIGH))
    _, _, inverse0 = factor_of(start[:R, :R], R)
    xs[:R, :] = dot32(inverse0, q_ref[...])

    def step(k, carry):
        for b in range(B):
            blocks[b] = xs[:R, b * BS : (b + 1) * BS]
        for d in range(W):
            for c in range(C):
                value = blocks[local[d * C + c]]
                (rb if d == 0 else sb)[pl.ds((d * C + c) * R, R), :] = value
            if d:
                request(d).start()

        def group(d, carry):
            @pl.when(d > 0)
            def _():
                request(d).wait_recv()

            for c in range(C):
                p = d * C + c
                rows = pl.ds(pl.multiple_of(p * R, R), R)
                tile = tiles[p]
                high, low = split(rb[rows, :])
                left = jnp.concatenate(
                    [
                        jnp.concatenate([high, high], axis=1),
                        jnp.concatenate([low, jnp.zeros_like(low)], axis=1),
                    ],
                    axis=0,
                )
                both = dot_nt(left, tile)
                tf[rows, :] = both[:R] + both[R:]
                high, low = split(blocks[first[p]])
                both = jnp.dot(
                    jnp.concatenate([high, low], axis=0), tile, preferred_element_type=jnp.float32
                )
                sb2[rows, :] = both[:R, :BS] + both[R:, :BS] + both[:R, BS:]

            @pl.when(d > 0)
            def _():
                answer(d).start()

            return carry

        lax.fori_loop(0, W, group, 0)
        rb2[pl.ds(0, CR), :] = sb2[pl.ds(0, CR), :]
        for d in range(1, W):
            answer(d).wait_recv()

        one_hot = owners[...]
        for n in range(1, N + 1):
            part = lax.rem(nar + n, N)
            for q in range(RN):
                r = part * RN + q
                x = jnp.concatenate(
                    [tf[pl.ds(r, W * C, stride=R), :], rb2[pl.ds(r, W * C, stride=R), :]], axis=0
                )
                high, low = split(x)
                value = jnp.dot(
                    one_hot,
                    jnp.concatenate([high, low], axis=0),
                    preferred_element_type=jnp.float32,
                )
                if n == N:
                    rs[0, pl.ds(q * B, B), :] = value
                else:
                    pb[pl.ds(pl.multiple_of(part * PR + q * B, B), B), :] = value
            if n < N:
                scatter(n).start()
        for d in range(1, N):
            scatter(d).wait_recv()
        mine = rs[0]
        for d in range(1, N):
            mine += rs[d]
        rs[0] = mine
        for d in range(1, N):
            gather(d).start()
        ag[pl.ds(pl.multiple_of(nar * PR, PR), PR), :] = mine
        for d in range(1, N):
            gathered(d).wait_recv()

        for b in range(B):
            xs[R:, b * BS : (b + 1) * BS] = ag[pl.ds(b, R, stride=B), :]
        xs[R:, :] = xs[R:, :] - dot32(up[...], prev[...])
        summed = gram_sum(dot_nt(xs[...], xs[...], HIGH))
        basis_gram = summed[:R, :R]
        along = summed[:R, R:]
        along_t = summed[R:, :R]
        raw = summed[R:, R:]
        gram = raw - 2.0 * dot32(along_t, along) + dot32(along_t, dot32(basis_gram, along))
        lower, upper, inverse = factor_of(gram, R)
        coef[k, 0] = along
        coef[k, 1] = lower
        prev[...] = xs[:R, :]
        up[...] = upper
        mix = jnp.concatenate([-dot32(inverse, along_t), inverse], axis=1)
        xs[:R, :] = dot32(mix, xs[...])

        for d in range(1, W):
            request(d).wait_send()
            answer(d).wait_send()
        for d in range(1, N):
            scatter(d).wait_send()
            gather(d).wait_send()
        return carry

    lax.fori_loop(0, STEPS, step, 0)
    out[...] = xs[:R, :]


def spread_kernel(dims, first, second, asked, unit, tiles, *scratch):
    W, N, C, B = dims
    Z = W // 2
    reach = Z - 1
    bufs = (scratch[:reach], scratch[reach : 2 * reach])
    out_buf, in_buf, sz, rz, sy, ry, sc, rc, sx, rx = scratch[2 * reach :]
    me = lax.axis_index("wide")
    nar = lax.axis_index("narrow")
    z, x = lax.div(me, 2), lax.rem(me, 2)
    across = me + 1 - 2 * x
    over = lax.rem(nar + 2, N)
    core = nar + 1 - 2 * lax.rem(nar, 2)
    core_over = lax.rem(core + 2, N)
    BQ = B // N

    def valid(t, g):
        return (z >= t) if g == 0 else (z + t < Z)

    def room(g):
        return (z + 1 < Z) if g == 0 else (z > 0)

    def held(t, g):
        return unit if t == 0 else bufs[g][t - 1]

    def quarter(ref, q):
        return ref.at[pl.ds(q * BQ, BQ)]

    def remote(src, dst, send, recv, where):
        return pltpu.make_async_remote_copy(
            src_ref=src, dst_ref=dst, send_sem=send, recv_sem=recv,
            device_id=where, device_id_type=MESH,
        )

    def along(t, g):
        return remote(
            quarter(held(t, g), nar), quarter(held(t + 1, g), nar),
            sz.at[g, t], rz.at[g, t + 1], {"wide": me + 2 if g == 0 else me - 2},
        )

    def arrived(t, g):
        part = quarter(held(t, g), nar)
        return remote(
            part, part, sz.at[g, t - 1], rz.at[g, t], {"wide": me + 2 if g == 0 else me - 2}
        )

    def sideways(t, g, q):
        part = quarter(held(t, g), q)
        return remote(part, part, sy.at[g, t], ry.at[g, t], {"narrow": over})

    def inside(t, g, j, q):
        part = quarter(held(t, g), q)
        return remote(part, part, sc.at[j, g, t], rc.at[j, g, t], {"narrow": core})

    def place(t, g):
        return g * reach + t

    def cross(t, g):
        k = place(t, g)
        return remote(out_buf.at[k], in_buf.at[k], sx.at[k], rx.at[k], {"wide": across})

    def group_of(t, g):
        return z - t if g == 0 else z + t

    def serve(t, g):
        o = 2 * group_of(t, g) + x
        for c in range(C):
            out_buf[place(t, g), c] = held(t, g)[asked[o * C + c]]
        cross(t, g).start()

    def make(o, load):
        slot = lax.rem(me - o + W, W)
        for c in range(C):
            s = dot_nt(unit[first[slot * C + c]], load(o, c))
            high, low = split(jnp.exp(KERNEL_FACTOR * (s - 1.0)))
            tiles[slot * C + c, :, :BS] = high
            tiles[slot * C + c, :, BS:] = low

    def near_tiles(t, g):
        make(2 * group_of(t, g) + x, lambda o, c: held(t, g)[second[o * C + c]])

    def far_tiles(t, g):
        cross(t, g).wait_recv()
        make(2 * group_of(t, g) + 1 - x, lambda o, c: in_buf[place(t, g), c])

    barrier = pltpu.get_barrier_semaphore()
    for where in ({"wide": across}, {"narrow": over}, {"narrow": core}):
        pl.semaphore_signal(barrier, inc=1, device_id=where, device_id_type=MESH)
    for g in range(2):
        @pl.when(room(g))
        def _():
            pl.semaphore_signal(
                barrier, inc=1, device_id={"wide": me + 2 if g == 0 else me - 2},
                device_id_type=MESH,
            )
    pl.semaphore_wait(barrier, 3 + jnp.minimum(z, 1) + jnp.minimum(Z - 1 - z, 1))

    for g in range(2):
        @pl.when(room(g))
        def _():
            along(0, g).start()
    serve(0, 0)
    near_tiles(0, 0)

    for t in range(1, Z + 1):
        if t < Z:
            for g in range(2):
                @pl.when(valid(t, g))
                def _():
                    arrived(t, g).wait_recv()

                    @pl.when(room(g))
                    def _():
                        if t + 1 < Z:
                            along(t, g).start()

                    sideways(t, g, nar).start()
                    inside(t, g, 0, nar).start()
        if t > 1:
            for g in range(2):
                @pl.when(valid(t - 1, g))
                def _():
                    sideways(t - 1, g, over).wait_recv()
                    inside(t - 1, g, 1, over).start()
                    inside(t - 1, g, 0, core).wait_recv()
                    inside(t - 1, g, 1, core_over).wait_recv()
                    serve(t - 1, g)
            for g in range(2):
                @pl.when(valid(t - 1, g))
                def _():
                    near_tiles(t - 1, g)
            if t == 2:
                far_tiles(0, 0)
    for t in range(1, Z):
        for g in range(2):
            @pl.when(valid(t, g))
            def _():
                far_tiles(t, g)

    cross(0, 0).wait_send()
    for t in range(Z):
        for g in range(2):
            if t:
                @pl.when(valid(t, g))
                def _():
                    sideways(t, g, nar).wait_send()
                    inside(t, g, 0, nar).wait_send()
                    inside(t, g, 1, over).wait_send()
                    cross(t, g).wait_send()

            if t + 1 < Z:
                @pl.when(valid(t, g) & room(g))
                def _():
                    along(t, g).wait_send()


def spread_tiles(first, second, asked, unit, wide_count, narrow_count):
    own_blocks, _, width = unit.shape
    pair_count = first.shape[0]
    C = pair_count // wide_count
    Z = wide_count // 2
    vmem = pl.BlockSpec(memory_space=pltpu.VMEM)
    smem = pl.BlockSpec(memory_space=pltpu.SMEM)
    half = pltpu.SemaphoreType.DMA((2, Z))
    full = pltpu.SemaphoreType.DMA((2, 2, Z))
    flat = pltpu.SemaphoreType.DMA((2 * Z - 1,))
    ends = pltpu.VMEM((2 * Z - 1, C, BS, width), jnp.bfloat16)
    return pl.pallas_call(
        functools.partial(spread_kernel, (wide_count, narrow_count, C, own_blocks)),
        out_shape=jax.ShapeDtypeStruct((pair_count, BS, 2 * BS), jnp.bfloat16),
        in_specs=[smem, smem, smem, vmem],
        out_specs=vmem,
        scratch_shapes=[pltpu.VMEM(unit.shape, jnp.bfloat16)] * (2 * Z - 2)
        + [ends, ends, half, half, half, half, full, full, flat, flat],
        compiler_params=pltpu.CompilerParams(collective_id=1, has_side_effects=True),
        name="spread",
    )(first, second, asked, unit)


SPREAD_BYTES = 16 * 2**20


def lanczos(first, local, owners, tiles, q_init, wide_count, narrow_count, total):
    R, cols = q_init.shape
    B = cols // BS
    pair_count = first.shape[0]
    C = pair_count // wide_count
    dims = (wide_count, narrow_count, C, R, B, total)
    vmem = pl.BlockSpec(memory_space=pltpu.VMEM)
    smem = pl.BlockSpec(memory_space=pltpu.SMEM)
    f32 = jnp.float32
    pairs_buf = pltpu.VMEM((pair_count * R, BS), f32)
    part = R // narrow_count * B
    wide_sem = pltpu.SemaphoreType.DMA((wide_count,))
    narrow_sem = pltpu.SemaphoreType.DMA((narrow_count,))
    return pl.pallas_call(
        functools.partial(main_kernel, dims),
        out_shape=(
            jax.ShapeDtypeStruct((R, cols), f32),
            jax.ShapeDtypeStruct((STEPS, 2, R, R), f32),
        ),
        in_specs=[smem, smem, vmem, vmem, vmem],
        out_specs=(vmem, vmem),
        scratch_shapes=[
            pairs_buf, pairs_buf, pairs_buf, pairs_buf, pairs_buf,
            pltpu.VMEM((R * B, BS), f32),
            pltpu.VMEM((narrow_count, part, BS), f32),
            pltpu.VMEM((R * B, BS), f32),
            pltpu.VMEM((2 * R, cols), f32),
            pltpu.VMEM((B, R, BS), f32),
            pltpu.VMEM((R, cols), f32),
            pltpu.VMEM((R, R), f32),
            pltpu.VMEM((2 * R, BS), f32),
            pltpu.VMEM((wide_count, 2 * R, BS), f32),
            wide_sem, wide_sem, wide_sem, wide_sem,
            narrow_sem, narrow_sem, narrow_sem, narrow_sem,
            wide_sem, wide_sem,
        ],
        compiler_params=pltpu.CompilerParams(collective_id=0, has_side_effects=True),
        name="lanczos",
    )(first, local, owners, tiles, q_init)


def per_device(points, q_init, pairs):
    wide_count = lax.axis_size("wide")
    narrow_count = lax.axis_size("narrow")
    me = lax.axis_index("wide")
    own_blocks = points.shape[0] // BS
    width = points.shape[1]
    pair_count = pairs.shape[1]
    capacity = pair_count // wide_count
    total = own_blocks * BS * wide_count
    unit = unit_rows(points).reshape(own_blocks, BS, width)
    turn = jnp.arange(wide_count, dtype=jnp.int32)
    first_rows = (pairs[0] - me * own_blocks).reshape(wide_count, capacity)
    first = first_rows[(me - turn) % wide_count].reshape(pair_count)
    second = (pairs[1].reshape(wide_count, capacity) - turn[:, None] * own_blocks)
    every = lax.all_to_all(
        jnp.broadcast_to(second.reshape(1, pair_count), (wide_count, pair_count)),
        "wide", split_axis=0, concat_axis=0, tiled=True,
    ).reshape(wide_count, wide_count, capacity)
    local_ids = lax.dynamic_index_in_dim(every, me, axis=1, keepdims=False)
    local = local_ids[(me + turn) % wide_count].reshape(pair_count)
    targets = jnp.concatenate([first, local, first, local])
    owners = (jnp.arange(own_blocks, dtype=jnp.int32)[:, None] == targets[None, :]).astype(
        jnp.bfloat16
    )
    buffers = (wide_count - 2) * unit.size * 2
    if wide_count % 2 == 0 and wide_count > 2 and narrow_count == 4 and buffers <= SPREAD_BYTES:
        asked = lax.dynamic_index_in_dim(every, me + 1 - 2 * (me % 2), axis=0, keepdims=False)
        tiles = spread_tiles(
            first, second.reshape(pair_count), asked.reshape(pair_count), unit,
            wide_count, narrow_count,
        )
    else:
        blocks = lax.all_to_all(
            unit[local_ids.reshape(pair_count)], "wide", split_axis=0, concat_axis=0, tiled=True
        ).reshape(wide_count, capacity, BS, width)
        tiles = make_tiles(jnp.reshape(me, (1,)).astype(jnp.int32), first, unit, blocks)
    return lanczos(first, local, owners, tiles, q_init, wide_count, narrow_count, total)


def solution(mesh):
    placed = (P("wide", None), P(None, "wide"), P(None, ("wide", "narrow")))
    return jax.shard_map(
        per_device, mesh=mesh, in_specs=placed, out_specs=(P(None, "wide"), P()), check_vma=False
    )
```

```python
import functools

import jax
import jax.numpy as jnp
from jax import lax
from jax.experimental import pallas as pl
from jax.experimental.pallas import tpu as pltpu
from jax.sharding import PartitionSpec as P

BS = 128
STEPS = 3
LEVELS = 32767.0
KERNEL_FACTOR = 3.0
EPSILON = 1e-06
HIGH = lax.Precision.HIGHEST
MESH = pl.DeviceIdType.MESH


def unit_rows(points):
    wide32 = points.astype(jnp.float32)
    scaled = wide32 * lax.rsqrt(jnp.sum(wide32 * wide32, axis=-1, keepdims=True) + EPSILON)
    return scaled.astype(jnp.bfloat16)


def split(x):
    high = x.astype(jnp.bfloat16)
    return high, (x - high.astype(jnp.float32)).astype(jnp.bfloat16)


def coded(x):
    top = jnp.maximum(jnp.max(jnp.abs(x), axis=1, keepdims=True), 1e-30)
    scaled = jnp.clip(jnp.round(x * (LEVELS / top)), -LEVELS, LEVELS)
    return scaled.astype(jnp.int32).astype(jnp.int16), top * (1.0 / LEVELS)


def number(x):
    return x.astype(jnp.int32).astype(jnp.float32)


def dot32(a, b):
    return jnp.dot(a, b, precision=HIGH, preferred_element_type=jnp.float32)


def dot_nt(a, b, precision=None):
    return lax.dot_general(
        a, b, (((1,), (1,)), ((), ())), precision=precision, preferred_element_type=jnp.float32
    )


def tiles_kernel(capacity, me_ref, first_ref, unit_ref, second_ref, out_ref):
    d = pl.program_id(0)
    for c in range(capacity):
        s = dot_nt(unit_ref[first_ref[d * capacity + c]], second_ref[0, c])
        high, low = split(jnp.exp(KERNEL_FACTOR * (s - 1.0)))
        out_ref[c, :, :BS] = high
        out_ref[c, :, BS:] = low


def make_tiles(me, first, unit, second):
    wide_count, capacity, _, width = second.shape
    own_blocks = unit.shape[0]
    spec = pltpu.PrefetchScalarGridSpec(
        num_scalar_prefetch=2,
        grid=(wide_count,),
        in_specs=[
            pl.BlockSpec((own_blocks, BS, width), lambda d, m, f: (0, 0, 0)),
            pl.BlockSpec(
                (1, capacity, BS, width),
                lambda d, m, f: (lax.rem(m[0] - d + wide_count, wide_count), 0, 0, 0),
            ),
        ],
        out_specs=pl.BlockSpec((capacity, BS, 2 * BS), lambda d, m, f: (d, 0, 0)),
    )
    return pl.pallas_call(
        functools.partial(tiles_kernel, capacity),
        grid_spec=spec,
        out_shape=jax.ShapeDtypeStruct((wide_count * capacity, BS, 2 * BS), jnp.bfloat16),
        name="tiles",
    )(me, first, unit, second)


def factor_of(gram, r):
    i = lax.broadcasted_iota(jnp.int32, (r, r), 0)
    j = lax.broadcasted_iota(jnp.int32, (r, r), 1)
    both_i = lax.broadcasted_iota(jnp.int32, (r, 2 * r), 0)
    m = jnp.concatenate([gram, (i == j).astype(jnp.float32)], axis=1)
    lower = jnp.zeros((r, r), jnp.float32)
    for k in range(r):
        inv = 1.0 / jnp.sqrt(m[k : k + 1, k : k + 1])
        row = m[k : k + 1, :] * inv
        col = m[:, k : k + 1] * inv
        lower = jnp.where((j == k) & (i >= k), col, lower)
        m = jnp.where(both_i == k, row, jnp.where(both_i > k, m - col * row, m))
    upper = jnp.where(j >= i, m[:, :r], 0.0)
    inverse = jnp.where(j <= i, m[:, r:], 0.0)
    return lower, upper, inverse


def main_kernel(
    dims, first, local, owners, tiles, q_ref, out, coef,
    sb, rb, sb2, rq, ss, rs1, ss2, rs2, coded_blocks, scales, rb2, tf, pb, rs, ag, xs, blocks, prev, up, gs, gr,
    s1, r1, s2, r2, s3, r3, s4, r4, s5, r5, s6, r6, s7, r7,
):
    W, N, C, R, B, total = dims
    CR = C * R
    RN = R // N
    PR = RN * B
    me = lax.axis_index("wide")
    nar = lax.axis_index("narrow")

    def up_peer(d):
        return lax.rem(me + d, W)

    def down_peer(d):
        return lax.rem(me - d + W, W)

    barrier = pltpu.get_barrier_semaphore()
    for d in range(1, W):
        pl.semaphore_signal(barrier, inc=1, device_id={"wide": up_peer(d)}, device_id_type=MESH)
    for d in range(1, N):
        pl.semaphore_signal(
            barrier, inc=1, device_id={"narrow": lax.rem(nar + d, N)}, device_id_type=MESH
        )
    pl.semaphore_wait(barrier, W - 1 + N - 1)

    def request(d):
        rows = pl.ds(d * CR, CR)
        return pltpu.make_async_remote_copy(
            src_ref=sb.at[rows], dst_ref=rb.at[rows], send_sem=s1.at[d], recv_sem=r1.at[d],
            device_id={"wide": up_peer(d)}, device_id_type=MESH,
        )

    def answer(d):
        rows = pl.ds(d * CR, CR)
        return pltpu.make_async_remote_copy(
            src_ref=sb2.at[rows], dst_ref=rq.at[rows], send_sem=s2.at[d], recv_sem=r2.at[d],
            device_id={"wide": down_peer(d)}, device_id_type=MESH,
        )

    def request_scale(d):
        rows = pl.ds(d * R, R)
        return pltpu.make_async_remote_copy(
            src_ref=ss.at[rows], dst_ref=rs1.at[rows], send_sem=s6.at[d], recv_sem=r6.at[d],
            device_id={"wide": up_peer(d)}, device_id_type=MESH,
        )

    def answer_scale(d):
        rows = pl.ds(d * R, R)
        return pltpu.make_async_remote_copy(
            src_ref=ss2.at[rows], dst_ref=rs2.at[rows], send_sem=s7.at[d], recv_sem=r7.at[d],
            device_id={"wide": down_peer(d)}, device_id_type=MESH,
        )

    lane = lax.broadcasted_iota(jnp.int32, (R, BS), 1)

    def scatter(d):
        return pltpu.make_async_remote_copy(
            src_ref=pb.at[pl.ds(lax.rem(nar + d, N) * PR, PR)], dst_ref=rs.at[d],
            send_sem=s3.at[d], recv_sem=r3.at[d],
            device_id={"narrow": lax.rem(nar + d, N)}, device_id_type=MESH,
        )

    def gather(d):
        mine = pl.ds(nar * PR, PR)
        return pltpu.make_async_remote_copy(
            src_ref=rs.at[0], dst_ref=ag.at[mine], send_sem=s4.at[d], recv_sem=r4.at[d],
            device_id={"narrow": lax.rem(nar + d, N)}, device_id_type=MESH,
        )

    def gathered(d):
        theirs = pl.ds(lax.rem(nar - d + N, N) * PR, PR)
        return pltpu.make_async_remote_copy(
            src_ref=rs.at[0], dst_ref=ag.at[theirs], send_sem=s4.at[d], recv_sem=r4.at[d],
            device_id={"narrow": lax.rem(nar + d, N)}, device_id_type=MESH,
        )

    def gram_copy(d):
        return pltpu.make_async_remote_copy(
            src_ref=gs, dst_ref=gr.at[d], send_sem=s5.at[d], recv_sem=r5.at[d],
            device_id={"wide": up_peer(d)}, device_id_type=MESH,
        )

    def gram_sum(value):
        gs[:, : 2 * R] = value
        gr[0, :, : 2 * R] = value
        for d in range(1, W):
            gram_copy(d).start()
        for d in range(1, W):
            gram_copy(d).wait_recv()
        summed = jnp.zeros((2 * R, 2 * R), jnp.float32)
        for s in range(W):
            summed += gr[lax.rem(me - s + W, W)][:, : 2 * R]
        for d in range(1, W):
            gram_copy(d).wait_send()
        return summed / total

    gs[...] = jnp.zeros_like(gs)
    xs[:R, :] = q_ref[...]
    xs[R:, :] = jnp.zeros((R, B * BS), jnp.float32)
    prev[...] = jnp.zeros_like(prev)
    up[...] = jnp.zeros_like(up)
    start = gram_sum(dot_nt(xs[...], xs[...], HIGH))
    _, _, inverse0 = factor_of(start[:R, :R], R)
    xs[:R, :] = dot32(inverse0, q_ref[...])

    def step(k, carry):
        for b in range(B):
            value = xs[:R, b * BS : (b + 1) * BS]
            blocks[b] = value
            whole, unit_of = coded(value)
            coded_blocks[b] = whole
            scales[b] = jnp.broadcast_to(unit_of, (R, BS))
        for d in range(W):
            spread = jnp.zeros((R, BS), jnp.float32)
            for c in range(C):
                value = coded_blocks[local[d * C + c]]
                (rb if d == 0 else sb)[pl.ds((d * C + c) * R, R), :] = value
                spread = jnp.where(lane == c, scales[local[d * C + c]], spread)
            (rs1 if d == 0 else ss)[pl.ds(d * R, R), :] = spread
            if d:
                request(d).start()
                request_scale(d).start()

        def group(d, carry):
            @pl.when(d > 0)
            def _():
                request(d).wait_recv()
                request_scale(d).wait_recv()

            scale_rows = pl.ds(pl.multiple_of(d * R, R), R)
            scale = rs1[scale_rows, :]
            spread = jnp.zeros((R, BS), jnp.float32)
            for c in range(C):
                p = d * C + c
                rows = pl.ds(pl.multiple_of(p * R, R), R)
                tile = tiles[p]
                high, low = split(number(rb[rows, :]))
                left = jnp.concatenate(
                    [
                        jnp.concatenate([high, high], axis=1),
                        jnp.concatenate([low, jnp.zeros_like(low)], axis=1),
                    ],
                    axis=0,
                )
                both = dot_nt(left, tile)
                tf[rows, :] = (both[:R] + both[R:]) * scale[:, c : c + 1]
                high, low = split(blocks[first[p]])
                both = jnp.dot(
                    jnp.concatenate([high, low], axis=0), tile, preferred_element_type=jnp.float32
                )
                whole, unit_of = coded(both[:R, :BS] + both[R:, :BS] + both[:R, BS:])
                sb2[rows, :] = whole
                spread = jnp.where(lane == c, unit_of, spread)
            ss2[scale_rows, :] = spread

            @pl.when(d > 0)
            def _():
                answer(d).start()
                answer_scale(d).start()

            return carry

        lax.fori_loop(0, W, group, 0)
        for d in range(W):
            if d:
                answer(d).wait_recv()
                answer_scale(d).wait_recv()
            scale = (rs2 if d else ss2)[pl.ds(d * R, R), :]
            for c in range(C):
                rows = pl.ds((d * C + c) * R, R)
                rb2[rows, :] = number((rq if d else sb2)[rows, :]) * scale[:, c : c + 1]

        one_hot = owners[...]
        for n in range(1, N + 1):
            part = lax.rem(nar + n, N)
            for q in range(RN):
                r = part * RN + q
                x = jnp.concatenate(
                    [tf[pl.ds(r, W * C, stride=R), :], rb2[pl.ds(r, W * C, stride=R), :]], axis=0
                )
                high, low = split(x)
                value = jnp.dot(
                    one_hot,
                    jnp.concatenate([high, low], axis=0),
                    preferred_element_type=jnp.float32,
                )
                if n == N:
                    rs[0, pl.ds(q * B, B), :] = value
                else:
                    pb[pl.ds(pl.multiple_of(part * PR + q * B, B), B), :] = value
            if n < N:
                scatter(n).start()
        for d in range(1, N):
            scatter(d).wait_recv()
        mine = rs[0]
        for d in range(1, N):
            mine += rs[d]
        rs[0] = mine
        for d in range(1, N):
            gather(d).start()
        ag[pl.ds(pl.multiple_of(nar * PR, PR), PR), :] = mine
        for d in range(1, N):
            gathered(d).wait_recv()

        for b in range(B):
            xs[R:, b * BS : (b + 1) * BS] = ag[pl.ds(b, R, stride=B), :]
        xs[R:, :] = xs[R:, :] - dot32(up[...], prev[...])
        summed = gram_sum(dot_nt(xs[...], xs[...], HIGH))
        basis_gram = summed[:R, :R]
        along = summed[:R, R:]
        along_t = summed[R:, :R]
        raw = summed[R:, R:]
        gram = raw - 2.0 * dot32(along_t, along) + dot32(along_t, dot32(basis_gram, along))
        lower, upper, inverse = factor_of(gram, R)
        coef[k, 0] = along
        coef[k, 1] = lower
        prev[...] = xs[:R, :]
        up[...] = upper
        mix = jnp.concatenate([-dot32(inverse, along_t), inverse], axis=1)
        xs[:R, :] = dot32(mix, xs[...])

        for d in range(1, W):
            request(d).wait_send()
            answer(d).wait_send()
            request_scale(d).wait_send()
            answer_scale(d).wait_send()
        for d in range(1, N):
            scatter(d).wait_send()
            gather(d).wait_send()
        return carry

    lax.fori_loop(0, STEPS, step, 0)
    out[...] = xs[:R, :]


def spread_kernel(dims, first, second, asked, unit, tiles, *scratch):
    W, N, C, B = dims
    Z = W // 2
    reach = Z - 1
    bufs = (scratch[:reach], scratch[reach : 2 * reach])
    out_buf, in_buf, sz, rz, sy, ry, sc, rc, sx, rx = scratch[2 * reach :]
    me = lax.axis_index("wide")
    nar = lax.axis_index("narrow")
    z, x = lax.div(me, 2), lax.rem(me, 2)
    across = me + 1 - 2 * x
    over = lax.rem(nar + 2, N)
    core = nar + 1 - 2 * lax.rem(nar, 2)
    core_over = lax.rem(core + 2, N)
    BQ = B // N

    def valid(t, g):
        return (z >= t) if g == 0 else (z + t < Z)

    def room(g):
        return (z + 1 < Z) if g == 0 else (z > 0)

    def held(t, g):
        return unit if t == 0 else bufs[g][t - 1]

    def quarter(ref, q):
        return ref.at[pl.ds(q * BQ, BQ)]

    def remote(src, dst, send, recv, where):
        return pltpu.make_async_remote_copy(
            src_ref=src, dst_ref=dst, send_sem=send, recv_sem=recv,
            device_id=where, device_id_type=MESH,
        )

    def along(t, g):
        return remote(
            quarter(held(t, g), nar), quarter(held(t + 1, g), nar),
            sz.at[g, t], rz.at[g, t + 1], {"wide": me + 2 if g == 0 else me - 2},
        )

    def arrived(t, g):
        part = quarter(held(t, g), nar)
        return remote(
            part, part, sz.at[g, t - 1], rz.at[g, t], {"wide": me + 2 if g == 0 else me - 2}
        )

    def sideways(t, g, q):
        part = quarter(held(t, g), q)
        return remote(part, part, sy.at[g, t], ry.at[g, t], {"narrow": over})

    def inside(t, g, j, q):
        part = quarter(held(t, g), q)
        return remote(part, part, sc.at[j, g, t], rc.at[j, g, t], {"narrow": core})

    def place(t, g):
        return g * reach + t

    def cross(t, g):
        k = place(t, g)
        return remote(out_buf.at[k], in_buf.at[k], sx.at[k], rx.at[k], {"wide": across})

    def group_of(t, g):
        return z - t if g == 0 else z + t

    def serve(t, g):
        o = 2 * group_of(t, g) + x
        for c in range(C):
            out_buf[place(t, g), c] = held(t, g)[asked[o * C + c]]
        cross(t, g).start()

    def make(o, load):
        slot = lax.rem(me - o + W, W)
        for c in range(C):
            s = dot_nt(unit[first[slot * C + c]], load(o, c))
            high, low = split(jnp.exp(KERNEL_FACTOR * (s - 1.0)))
            tiles[slot * C + c, :, :BS] = high
            tiles[slot * C + c, :, BS:] = low

    def near_tiles(t, g):
        make(2 * group_of(t, g) + x, lambda o, c: held(t, g)[second[o * C + c]])

    def far_tiles(t, g):
        cross(t, g).wait_recv()
        make(2 * group_of(t, g) + 1 - x, lambda o, c: in_buf[place(t, g), c])

    barrier = pltpu.get_barrier_semaphore()
    for where in ({"wide": across}, {"narrow": over}, {"narrow": core}):
        pl.semaphore_signal(barrier, inc=1, device_id=where, device_id_type=MESH)
    for g in range(2):
        @pl.when(room(g))
        def _():
            pl.semaphore_signal(
                barrier, inc=1, device_id={"wide": me + 2 if g == 0 else me - 2},
                device_id_type=MESH,
            )
    pl.semaphore_wait(barrier, 3 + jnp.minimum(z, 1) + jnp.minimum(Z - 1 - z, 1))

    for g in range(2):
        @pl.when(room(g))
        def _():
            along(0, g).start()
    serve(0, 0)
    near_tiles(0, 0)

    for t in range(1, Z + 1):
        if t < Z:
            for g in range(2):
                @pl.when(valid(t, g))
                def _():
                    arrived(t, g).wait_recv()

                    @pl.when(room(g))
                    def _():
                        if t + 1 < Z:
                            along(t, g).start()

                    sideways(t, g, nar).start()
                    inside(t, g, 0, nar).start()
        if t > 1:
            for g in range(2):
                @pl.when(valid(t - 1, g))
                def _():
                    sideways(t - 1, g, over).wait_recv()
                    inside(t - 1, g, 1, over).start()
                    inside(t - 1, g, 0, core).wait_recv()
                    inside(t - 1, g, 1, core_over).wait_recv()
                    serve(t - 1, g)
            for g in range(2):
                @pl.when(valid(t - 1, g))
                def _():
                    near_tiles(t - 1, g)
            if t == 2:
                far_tiles(0, 0)
    for t in range(1, Z):
        for g in range(2):
            @pl.when(valid(t, g))
            def _():
                far_tiles(t, g)

    cross(0, 0).wait_send()
    for t in range(Z):
        for g in range(2):
            if t:
                @pl.when(valid(t, g))
                def _():
                    sideways(t, g, nar).wait_send()
                    inside(t, g, 0, nar).wait_send()
                    inside(t, g, 1, over).wait_send()
                    cross(t, g).wait_send()

            if t + 1 < Z:
                @pl.when(valid(t, g) & room(g))
                def _():
                    along(t, g).wait_send()


def spread_tiles(first, second, asked, unit, wide_count, narrow_count):
    own_blocks, _, width = unit.shape
    pair_count = first.shape[0]
    C = pair_count // wide_count
    Z = wide_count // 2
    vmem = pl.BlockSpec(memory_space=pltpu.VMEM)
    smem = pl.BlockSpec(memory_space=pltpu.SMEM)
    half = pltpu.SemaphoreType.DMA((2, Z))
    full = pltpu.SemaphoreType.DMA((2, 2, Z))
    flat = pltpu.SemaphoreType.DMA((2 * Z - 1,))
    ends = pltpu.VMEM((2 * Z - 1, C, BS, width), jnp.bfloat16)
    return pl.pallas_call(
        functools.partial(spread_kernel, (wide_count, narrow_count, C, own_blocks)),
        out_shape=jax.ShapeDtypeStruct((pair_count, BS, 2 * BS), jnp.bfloat16),
        in_specs=[smem, smem, smem, vmem],
        out_specs=vmem,
        scratch_shapes=[pltpu.VMEM(unit.shape, jnp.bfloat16)] * (2 * Z - 2)
        + [ends, ends, half, half, half, half, full, full, flat, flat],
        compiler_params=pltpu.CompilerParams(collective_id=1, has_side_effects=True),
        name="spread",
    )(first, second, asked, unit)


SPREAD_BYTES = 16 * 2**20


def lanczos(first, local, owners, tiles, q_init, wide_count, narrow_count, total):
    R, cols = q_init.shape
    B = cols // BS
    pair_count = first.shape[0]
    C = pair_count // wide_count
    dims = (wide_count, narrow_count, C, R, B, total)
    vmem = pl.BlockSpec(memory_space=pltpu.VMEM)
    smem = pl.BlockSpec(memory_space=pltpu.SMEM)
    f32 = jnp.float32
    pairs_buf = pltpu.VMEM((pair_count * R, BS), f32)
    coded_buf = pltpu.VMEM((pair_count * R, BS), jnp.int16)
    scale_buf = pltpu.VMEM((wide_count * R, BS), f32)
    part = R // narrow_count * B
    wide_sem = pltpu.SemaphoreType.DMA((wide_count,))
    narrow_sem = pltpu.SemaphoreType.DMA((narrow_count,))
    return pl.pallas_call(
        functools.partial(main_kernel, dims),
        out_shape=(
            jax.ShapeDtypeStruct((R, cols), f32),
            jax.ShapeDtypeStruct((STEPS, 2, R, R), f32),
        ),
        in_specs=[smem, smem, vmem, vmem, vmem],
        out_specs=(vmem, vmem),
        scratch_shapes=[
            coded_buf, coded_buf, coded_buf, coded_buf,
            scale_buf, scale_buf, scale_buf, scale_buf,
            pltpu.VMEM((B, R, BS), jnp.int16),
            pltpu.VMEM((B, R, BS), f32),
            pairs_buf, pairs_buf,
            pltpu.VMEM((R * B, BS), f32),
            pltpu.VMEM((narrow_count, part, BS), f32),
            pltpu.VMEM((R * B, BS), f32),
            pltpu.VMEM((2 * R, cols), f32),
            pltpu.VMEM((B, R, BS), f32),
            pltpu.VMEM((R, cols), f32),
            pltpu.VMEM((R, R), f32),
            pltpu.VMEM((2 * R, BS), f32),
            pltpu.VMEM((wide_count, 2 * R, BS), f32),
            wide_sem, wide_sem, wide_sem, wide_sem,
            narrow_sem, narrow_sem, narrow_sem, narrow_sem,
            wide_sem, wide_sem, wide_sem, wide_sem, wide_sem, wide_sem,
        ],
        compiler_params=pltpu.CompilerParams(collective_id=0, has_side_effects=True),
        name="lanczos",
    )(first, local, owners, tiles, q_init)


def per_device(points, q_init, pairs):
    wide_count = lax.axis_size("wide")
    narrow_count = lax.axis_size("narrow")
    me = lax.axis_index("wide")
    own_blocks = points.shape[0] // BS
    width = points.shape[1]
    pair_count = pairs.shape[1]
    capacity = pair_count // wide_count
    total = own_blocks * BS * wide_count
    unit = unit_rows(points).reshape(own_blocks, BS, width)
    turn = jnp.arange(wide_count, dtype=jnp.int32)
    first_rows = (pairs[0] - me * own_blocks).reshape(wide_count, capacity)
    first = first_rows[(me - turn) % wide_count].reshape(pair_count)
    second = (pairs[1].reshape(wide_count, capacity) - turn[:, None] * own_blocks)
    every = lax.all_to_all(
        jnp.broadcast_to(second.reshape(1, pair_count), (wide_count, pair_count)),
        "wide", split_axis=0, concat_axis=0, tiled=True,
    ).reshape(wide_count, wide_count, capacity)
    local_ids = lax.dynamic_index_in_dim(every, me, axis=1, keepdims=False)
    local = local_ids[(me + turn) % wide_count].reshape(pair_count)
    targets = jnp.concatenate([first, local, first, local])
    owners = (jnp.arange(own_blocks, dtype=jnp.int32)[:, None] == targets[None, :]).astype(
        jnp.bfloat16
    )
    buffers = (wide_count - 2) * unit.size * 2
    if wide_count % 2 == 0 and wide_count > 2 and narrow_count == 4 and buffers <= SPREAD_BYTES:
        asked = lax.dynamic_index_in_dim(every, me + 1 - 2 * (me % 2), axis=0, keepdims=False)
        tiles = spread_tiles(
            first, second.reshape(pair_count), asked.reshape(pair_count), unit,
            wide_count, narrow_count,
        )
    else:
        blocks = lax.all_to_all(
            unit[local_ids.reshape(pair_count)], "wide", split_axis=0, concat_axis=0, tiled=True
        ).reshape(wide_count, capacity, BS, width)
        tiles = make_tiles(jnp.reshape(me, (1,)).astype(jnp.int32), first, unit, blocks)
    return lanczos(first, local, owners, tiles, q_init, wide_count, narrow_count, total)


def solution(mesh):
    placed = (P("wide", None), P(None, "wide"), P(None, ("wide", "narrow")))
    return jax.shard_map(
        per_device, mesh=mesh, in_specs=placed, out_specs=(P(None, "wide"), P()), check_vma=False
    )
```

```python
import functools

import jax
import jax.numpy as jnp
from jax import lax
from jax.experimental import pallas as pl
from jax.experimental.pallas import tpu as pltpu
from jax.sharding import PartitionSpec as P

BS = 128
STEPS = 3
LEVELS = 32767.0
KERNEL_FACTOR = 3.0
EPSILON = 1e-06
HIGH = lax.Precision.HIGHEST
MESH = pl.DeviceIdType.MESH


def unit_rows(points):
    wide32 = points.astype(jnp.float32)
    scaled = wide32 * lax.rsqrt(jnp.sum(wide32 * wide32, axis=-1, keepdims=True) + EPSILON)
    return scaled.astype(jnp.bfloat16)


def split(x):
    high = x.astype(jnp.bfloat16)
    return high, (x - high.astype(jnp.float32)).astype(jnp.bfloat16)


def coded(x, axes=1):
    top = jnp.maximum(jnp.max(jnp.abs(x), axis=axes, keepdims=True), 1e-30)
    scaled = jnp.clip(jnp.round(x * (LEVELS / top)), -LEVELS, LEVELS)
    return scaled.astype(jnp.int32).astype(jnp.int16), top * (1.0 / LEVELS)


def number(x):
    return x.astype(jnp.int32).astype(jnp.float32)


def dot32(a, b):
    return jnp.dot(a, b, precision=HIGH, preferred_element_type=jnp.float32)


def dot_nt(a, b, precision=None):
    return lax.dot_general(
        a, b, (((1,), (1,)), ((), ())), precision=precision, preferred_element_type=jnp.float32
    )


def tiles_kernel(capacity, me_ref, first_ref, unit_ref, second_ref, out_ref):
    d = pl.program_id(0)
    for c in range(capacity):
        s = dot_nt(unit_ref[first_ref[d * capacity + c]], second_ref[0, c])
        high, low = split(jnp.exp(KERNEL_FACTOR * (s - 1.0)))
        out_ref[c, :, :BS] = high
        out_ref[c, :, BS:] = low


def make_tiles(me, first, unit, second):
    wide_count, capacity, _, width = second.shape
    own_blocks = unit.shape[0]
    spec = pltpu.PrefetchScalarGridSpec(
        num_scalar_prefetch=2,
        grid=(wide_count,),
        in_specs=[
            pl.BlockSpec((own_blocks, BS, width), lambda d, m, f: (0, 0, 0)),
            pl.BlockSpec(
                (1, capacity, BS, width),
                lambda d, m, f: (lax.rem(m[0] - d + wide_count, wide_count), 0, 0, 0),
            ),
        ],
        out_specs=pl.BlockSpec((capacity, BS, 2 * BS), lambda d, m, f: (d, 0, 0)),
    )
    return pl.pallas_call(
        functools.partial(tiles_kernel, capacity),
        grid_spec=spec,
        out_shape=jax.ShapeDtypeStruct((wide_count * capacity, BS, 2 * BS), jnp.bfloat16),
        name="tiles",
    )(me, first, unit, second)


def factor_of(gram, r):
    i = lax.broadcasted_iota(jnp.int32, (r, r), 0)
    j = lax.broadcasted_iota(jnp.int32, (r, r), 1)
    both_i = lax.broadcasted_iota(jnp.int32, (r, 2 * r), 0)
    m = jnp.concatenate([gram, (i == j).astype(jnp.float32)], axis=1)
    lower = jnp.zeros((r, r), jnp.float32)
    for k in range(r):
        inv = 1.0 / jnp.sqrt(m[k : k + 1, k : k + 1])
        row = m[k : k + 1, :] * inv
        col = m[:, k : k + 1] * inv
        lower = jnp.where((j == k) & (i >= k), col, lower)
        m = jnp.where(both_i == k, row, jnp.where(both_i > k, m - col * row, m))
    upper = jnp.where(j >= i, m[:, :r], 0.0)
    inverse = jnp.where(j <= i, m[:, r:], 0.0)
    return lower, upper, inverse


def main_kernel(
    dims, first, local, owners, tiles, q_ref, out, coef,
    sb, rb, sb2, rq, ss, rs1, ss2, rs2, coded_blocks, scales, rb2, tf, pb, rs, ag, acc, out16, all16, psc, rsc, osc, asc, xs, blocks, prev, up, gs, gr,
    s1, r1, s2, r2, s3, r3, s4, r4, s5, r5, s6, r6, s7, r7, s8, r8, s9, r9,
):
    W, N, C, R, B, total = dims
    CR = C * R
    RN = R // N
    PR = RN * B
    me = lax.axis_index("wide")
    nar = lax.axis_index("narrow")

    def up_peer(d):
        return lax.rem(me + d, W)

    def down_peer(d):
        return lax.rem(me - d + W, W)

    barrier = pltpu.get_barrier_semaphore()
    for d in range(1, W):
        pl.semaphore_signal(barrier, inc=1, device_id={"wide": up_peer(d)}, device_id_type=MESH)
    for d in range(1, N):
        pl.semaphore_signal(
            barrier, inc=1, device_id={"narrow": lax.rem(nar + d, N)}, device_id_type=MESH
        )
    pl.semaphore_wait(barrier, W - 1 + N - 1)

    def request(d):
        rows = pl.ds(d * CR, CR)
        return pltpu.make_async_remote_copy(
            src_ref=sb.at[rows], dst_ref=rb.at[rows], send_sem=s1.at[d], recv_sem=r1.at[d],
            device_id={"wide": up_peer(d)}, device_id_type=MESH,
        )

    def answer(d):
        rows = pl.ds(d * CR, CR)
        return pltpu.make_async_remote_copy(
            src_ref=sb2.at[rows], dst_ref=rq.at[rows], send_sem=s2.at[d], recv_sem=r2.at[d],
            device_id={"wide": down_peer(d)}, device_id_type=MESH,
        )

    def request_scale(d):
        rows = pl.ds(d * R, R)
        return pltpu.make_async_remote_copy(
            src_ref=ss.at[rows], dst_ref=rs1.at[rows], send_sem=s6.at[d], recv_sem=r6.at[d],
            device_id={"wide": up_peer(d)}, device_id_type=MESH,
        )

    def answer_scale(d):
        rows = pl.ds(d * R, R)
        return pltpu.make_async_remote_copy(
            src_ref=ss2.at[rows], dst_ref=rs2.at[rows], send_sem=s7.at[d], recv_sem=r7.at[d],
            device_id={"wide": down_peer(d)}, device_id_type=MESH,
        )

    lane = lax.broadcasted_iota(jnp.int32, (R, BS), 1)

    def scatter(d):
        return pltpu.make_async_remote_copy(
            src_ref=pb.at[pl.ds(lax.rem(nar + d, N) * PR, PR)], dst_ref=rs.at[d],
            send_sem=s3.at[d], recv_sem=r3.at[d],
            device_id={"narrow": lax.rem(nar + d, N)}, device_id_type=MESH,
        )

    def gather(d):
        mine = pl.ds(nar * PR, PR)
        return pltpu.make_async_remote_copy(
            src_ref=out16, dst_ref=all16.at[mine], send_sem=s4.at[d], recv_sem=r4.at[d],
            device_id={"narrow": lax.rem(nar + d, N)}, device_id_type=MESH,
        )

    def gathered(d):
        theirs = pl.ds(lax.rem(nar - d + N, N) * PR, PR)
        return pltpu.make_async_remote_copy(
            src_ref=out16, dst_ref=all16.at[theirs], send_sem=s4.at[d], recv_sem=r4.at[d],
            device_id={"narrow": lax.rem(nar + d, N)}, device_id_type=MESH,
        )

    def scatter_scale(d):
        return pltpu.make_async_remote_copy(
            src_ref=psc.at[d], dst_ref=rsc.at[d], send_sem=s8.at[d], recv_sem=r8.at[d],
            device_id={"narrow": lax.rem(nar + d, N)}, device_id_type=MESH,
        )

    def gather_scale(d, slot):
        return pltpu.make_async_remote_copy(
            src_ref=osc, dst_ref=asc.at[slot], send_sem=s9.at[d], recv_sem=r9.at[d],
            device_id={"narrow": lax.rem(nar + d, N)}, device_id_type=MESH,
        )

    lane8 = lax.broadcasted_iota(jnp.int32, (8, BS), 1)

    def gram_copy(d):
        return pltpu.make_async_remote_copy(
            src_ref=gs, dst_ref=gr.at[d], send_sem=s5.at[d], recv_sem=r5.at[d],
            device_id={"wide": up_peer(d)}, device_id_type=MESH,
        )

    def gram_sum(value):
        gs[:, : 2 * R] = value
        gr[0, :, : 2 * R] = value
        for d in range(1, W):
            gram_copy(d).start()
        for d in range(1, W):
            gram_copy(d).wait_recv()
        summed = jnp.zeros((2 * R, 2 * R), jnp.float32)
        for s in range(W):
            summed += gr[lax.rem(me - s + W, W)][:, : 2 * R]
        for d in range(1, W):
            gram_copy(d).wait_send()
        return summed / total

    gs[...] = jnp.zeros_like(gs)
    xs[:R, :] = q_ref[...]
    xs[R:, :] = jnp.zeros((R, B * BS), jnp.float32)
    prev[...] = jnp.zeros_like(prev)
    up[...] = jnp.zeros_like(up)
    start = gram_sum(dot_nt(xs[...], xs[...], HIGH))
    _, _, inverse0 = factor_of(start[:R, :R], R)
    xs[:R, :] = dot32(inverse0, q_ref[...])

    def step(k, carry):
        for b in range(B):
            value = xs[:R, b * BS : (b + 1) * BS]
            blocks[b] = value
            whole, unit_of = coded(value)
            coded_blocks[b] = whole
            scales[b] = jnp.broadcast_to(unit_of, (R, BS))
        for d in range(W):
            spread = jnp.zeros((R, BS), jnp.float32)
            for c in range(C):
                value = coded_blocks[local[d * C + c]]
                (rb if d == 0 else sb)[pl.ds((d * C + c) * R, R), :] = value
                spread = jnp.where(lane == c, scales[local[d * C + c]], spread)
            (rs1 if d == 0 else ss)[pl.ds(d * R, R), :] = spread
            if d:
                request(d).start()
                request_scale(d).start()

        def group(d, carry):
            @pl.when(d > 0)
            def _():
                request(d).wait_recv()
                request_scale(d).wait_recv()

            scale_rows = pl.ds(pl.multiple_of(d * R, R), R)
            scale = rs1[scale_rows, :]
            spread = jnp.zeros((R, BS), jnp.float32)
            for c in range(C):
                p = d * C + c
                rows = pl.ds(pl.multiple_of(p * R, R), R)
                tile = tiles[p]
                high, low = split(number(rb[rows, :]))
                left = jnp.concatenate(
                    [
                        jnp.concatenate([high, high], axis=1),
                        jnp.concatenate([low, jnp.zeros_like(low)], axis=1),
                    ],
                    axis=0,
                )
                both = dot_nt(left, tile)
                tf[rows, :] = (both[:R] + both[R:]) * scale[:, c : c + 1]
                high, low = split(blocks[first[p]])
                both = jnp.dot(
                    jnp.concatenate([high, low], axis=0), tile, preferred_element_type=jnp.float32
                )
                whole, unit_of = coded(both[:R, :BS] + both[R:, :BS] + both[:R, BS:])
                sb2[rows, :] = whole
                spread = jnp.where(lane == c, unit_of, spread)
            ss2[scale_rows, :] = spread

            @pl.when(d > 0)
            def _():
                answer(d).start()
                answer_scale(d).start()

            return carry

        lax.fori_loop(0, W, group, 0)
        for d in range(W):
            if d:
                answer(d).wait_recv()
                answer_scale(d).wait_recv()
            scale = (rs2 if d else ss2)[pl.ds(d * R, R), :]
            for c in range(C):
                rows = pl.ds((d * C + c) * R, R)
                rb2[rows, :] = number((rq if d else sb2)[rows, :]) * scale[:, c : c + 1]

        one_hot = owners[...]
        for n in range(1, N + 1):
            part = lax.rem(nar + n, N)
            spread = jnp.zeros((8, BS), jnp.float32)
            for q in range(RN):
                r = part * RN + q
                x = jnp.concatenate(
                    [tf[pl.ds(r, W * C, stride=R), :], rb2[pl.ds(r, W * C, stride=R), :]], axis=0
                )
                high, low = split(x)
                value = jnp.dot(
                    one_hot,
                    jnp.concatenate([high, low], axis=0),
                    preferred_element_type=jnp.float32,
                )
                if n == N:
                    acc[pl.ds(q * B, B), :] = value
                else:
                    whole, unit_of = coded(value, (0, 1))
                    pb[pl.ds(pl.multiple_of(part * PR + q * B, B), B), :] = whole
                    spread = jnp.where(lane8 == q, unit_of, spread)
            if n < N:
                psc[n] = spread
                scatter(n).start()
                scatter_scale(n).start()
        for d in range(1, N):
            scatter(d).wait_recv()
            scatter_scale(d).wait_recv()
        spread = jnp.zeros((8, BS), jnp.float32)
        for q in range(RN):
            rows = pl.ds(q * B, B)
            value = acc[rows, :]
            for d in range(1, N):
                value += number(rs[d, rows, :]) * rsc[d][:1, q : q + 1]
            whole, unit_of = coded(value, (0, 1))
            out16[rows, :] = whole
            all16[pl.ds(pl.multiple_of(nar * PR + q * B, B), B), :] = whole
            spread = jnp.where(lane8 == q, unit_of, spread)
        osc[...] = spread
        asc[nar] = spread
        for d in range(1, N):
            gather(d).start()
            gather_scale(d, nar).start()
        for d in range(1, N):
            gathered(d).wait_recv()
            gather_scale(d, lax.rem(nar - d + N, N)).wait_recv()
        for r in range(R):
            rows = pl.ds(r * B, B)
            unit_of = asc[r // RN][:1, r % RN : r % RN + 1]
            ag[rows, :] = number(all16[rows, :]) * unit_of

        for b in range(B):
            xs[R:, b * BS : (b + 1) * BS] = ag[pl.ds(b, R, stride=B), :]
        xs[R:, :] = xs[R:, :] - dot32(up[...], prev[...])
        summed = gram_sum(dot_nt(xs[...], xs[...], HIGH))
        basis_gram = summed[:R, :R]
        along = summed[:R, R:]
        along_t = summed[R:, :R]
        raw = summed[R:, R:]
        gram = raw - 2.0 * dot32(along_t, along) + dot32(along_t, dot32(basis_gram, along))
        lower, upper, inverse = factor_of(gram, R)
        coef[k, 0] = along
        coef[k, 1] = lower
        prev[...] = xs[:R, :]
        up[...] = upper
        mix = jnp.concatenate([-dot32(inverse, along_t), inverse], axis=1)
        xs[:R, :] = dot32(mix, xs[...])

        for d in range(1, W):
            request(d).wait_send()
            answer(d).wait_send()
            request_scale(d).wait_send()
            answer_scale(d).wait_send()
        for d in range(1, N):
            scatter(d).wait_send()
            gather(d).wait_send()
            scatter_scale(d).wait_send()
            gather_scale(d, nar).wait_send()
        return carry

    lax.fori_loop(0, STEPS, step, 0)
    out[...] = xs[:R, :]


def spread_kernel(dims, first, second, asked, unit, tiles, *scratch):
    W, N, C, B = dims
    Z = W // 2
    reach = Z - 1
    bufs = (scratch[:reach], scratch[reach : 2 * reach])
    out_buf, in_buf, sz, rz, sy, ry, sc, rc, sx, rx = scratch[2 * reach :]
    me = lax.axis_index("wide")
    nar = lax.axis_index("narrow")
    z, x = lax.div(me, 2), lax.rem(me, 2)
    across = me + 1 - 2 * x
    over = lax.rem(nar + 2, N)
    core = nar + 1 - 2 * lax.rem(nar, 2)
    core_over = lax.rem(core + 2, N)
    BQ = B // N

    def valid(t, g):
        return (z >= t) if g == 0 else (z + t < Z)

    def room(g):
        return (z + 1 < Z) if g == 0 else (z > 0)

    def held(t, g):
        return unit if t == 0 else bufs[g][t - 1]

    def quarter(ref, q):
        return ref.at[pl.ds(q * BQ, BQ)]

    def remote(src, dst, send, recv, where):
        return pltpu.make_async_remote_copy(
            src_ref=src, dst_ref=dst, send_sem=send, recv_sem=recv,
            device_id=where, device_id_type=MESH,
        )

    def along(t, g):
        return remote(
            quarter(held(t, g), nar), quarter(held(t + 1, g), nar),
            sz.at[g, t], rz.at[g, t + 1], {"wide": me + 2 if g == 0 else me - 2},
        )

    def arrived(t, g):
        part = quarter(held(t, g), nar)
        return remote(
            part, part, sz.at[g, t - 1], rz.at[g, t], {"wide": me + 2 if g == 0 else me - 2}
        )

    def sideways(t, g, q):
        part = quarter(held(t, g), q)
        return remote(part, part, sy.at[g, t], ry.at[g, t], {"narrow": over})

    def inside(t, g, j, q):
        part = quarter(held(t, g), q)
        return remote(part, part, sc.at[j, g, t], rc.at[j, g, t], {"narrow": core})

    def place(t, g):
        return g * reach + t

    def cross(t, g):
        k = place(t, g)
        return remote(out_buf.at[k], in_buf.at[k], sx.at[k], rx.at[k], {"wide": across})

    def group_of(t, g):
        return z - t if g == 0 else z + t

    def serve(t, g):
        o = 2 * group_of(t, g) + x
        for c in range(C):
            out_buf[place(t, g), c] = held(t, g)[asked[o * C + c]]
        cross(t, g).start()

    def make(o, load):
        slot = lax.rem(me - o + W, W)
        for c in range(C):
            s = dot_nt(unit[first[slot * C + c]], load(o, c))
            high, low = split(jnp.exp(KERNEL_FACTOR * (s - 1.0)))
            tiles[slot * C + c, :, :BS] = high
            tiles[slot * C + c, :, BS:] = low

    def near_tiles(t, g):
        make(2 * group_of(t, g) + x, lambda o, c: held(t, g)[second[o * C + c]])

    def far_tiles(t, g):
        cross(t, g).wait_recv()
        make(2 * group_of(t, g) + 1 - x, lambda o, c: in_buf[place(t, g), c])

    barrier = pltpu.get_barrier_semaphore()
    for where in ({"wide": across}, {"narrow": over}, {"narrow": core}):
        pl.semaphore_signal(barrier, inc=1, device_id=where, device_id_type=MESH)
    for g in range(2):
        @pl.when(room(g))
        def _():
            pl.semaphore_signal(
                barrier, inc=1, device_id={"wide": me + 2 if g == 0 else me - 2},
                device_id_type=MESH,
            )
    pl.semaphore_wait(barrier, 3 + jnp.minimum(z, 1) + jnp.minimum(Z - 1 - z, 1))

    for g in range(2):
        @pl.when(room(g))
        def _():
            along(0, g).start()
    serve(0, 0)
    near_tiles(0, 0)

    for t in range(1, Z + 1):
        if t < Z:
            for g in range(2):
                @pl.when(valid(t, g))
                def _():
                    arrived(t, g).wait_recv()

                    @pl.when(room(g))
                    def _():
                        if t + 1 < Z:
                            along(t, g).start()

                    sideways(t, g, nar).start()
                    inside(t, g, 0, nar).start()
        if t > 1:
            for g in range(2):
                @pl.when(valid(t - 1, g))
                def _():
                    sideways(t - 1, g, over).wait_recv()
                    inside(t - 1, g, 1, over).start()
                    inside(t - 1, g, 0, core).wait_recv()
                    inside(t - 1, g, 1, core_over).wait_recv()
                    serve(t - 1, g)
            for g in range(2):
                @pl.when(valid(t - 1, g))
                def _():
                    near_tiles(t - 1, g)
            if t == 2:
                far_tiles(0, 0)
    for t in range(1, Z):
        for g in range(2):
            @pl.when(valid(t, g))
            def _():
                far_tiles(t, g)

    cross(0, 0).wait_send()
    for t in range(Z):
        for g in range(2):
            if t:
                @pl.when(valid(t, g))
                def _():
                    sideways(t, g, nar).wait_send()
                    inside(t, g, 0, nar).wait_send()
                    inside(t, g, 1, over).wait_send()
                    cross(t, g).wait_send()

            if t + 1 < Z:
                @pl.when(valid(t, g) & room(g))
                def _():
                    along(t, g).wait_send()


def spread_tiles(first, second, asked, unit, wide_count, narrow_count):
    own_blocks, _, width = unit.shape
    pair_count = first.shape[0]
    C = pair_count // wide_count
    Z = wide_count // 2
    vmem = pl.BlockSpec(memory_space=pltpu.VMEM)
    smem = pl.BlockSpec(memory_space=pltpu.SMEM)
    half = pltpu.SemaphoreType.DMA((2, Z))
    full = pltpu.SemaphoreType.DMA((2, 2, Z))
    flat = pltpu.SemaphoreType.DMA((2 * Z - 1,))
    ends = pltpu.VMEM((2 * Z - 1, C, BS, width), jnp.bfloat16)
    return pl.pallas_call(
        functools.partial(spread_kernel, (wide_count, narrow_count, C, own_blocks)),
        out_shape=jax.ShapeDtypeStruct((pair_count, BS, 2 * BS), jnp.bfloat16),
        in_specs=[smem, smem, smem, vmem],
        out_specs=vmem,
        scratch_shapes=[pltpu.VMEM(unit.shape, jnp.bfloat16)] * (2 * Z - 2)
        + [ends, ends, half, half, half, half, full, full, flat, flat],
        compiler_params=pltpu.CompilerParams(collective_id=1, has_side_effects=True),
        name="spread",
    )(first, second, asked, unit)


SPREAD_BYTES = 16 * 2**20


def lanczos(first, local, owners, tiles, q_init, wide_count, narrow_count, total):
    R, cols = q_init.shape
    B = cols // BS
    pair_count = first.shape[0]
    C = pair_count // wide_count
    dims = (wide_count, narrow_count, C, R, B, total)
    vmem = pl.BlockSpec(memory_space=pltpu.VMEM)
    smem = pl.BlockSpec(memory_space=pltpu.SMEM)
    f32 = jnp.float32
    pairs_buf = pltpu.VMEM((pair_count * R, BS), f32)
    coded_buf = pltpu.VMEM((pair_count * R, BS), jnp.int16)
    scale_buf = pltpu.VMEM((wide_count * R, BS), f32)
    part = R // narrow_count * B
    wide_sem = pltpu.SemaphoreType.DMA((wide_count,))
    narrow_sem = pltpu.SemaphoreType.DMA((narrow_count,))
    return pl.pallas_call(
        functools.partial(main_kernel, dims),
        out_shape=(
            jax.ShapeDtypeStruct((R, cols), f32),
            jax.ShapeDtypeStruct((STEPS, 2, R, R), f32),
        ),
        in_specs=[smem, smem, vmem, vmem, vmem],
        out_specs=(vmem, vmem),
        scratch_shapes=[
            coded_buf, coded_buf, coded_buf, coded_buf,
            scale_buf, scale_buf, scale_buf, scale_buf,
            pltpu.VMEM((B, R, BS), jnp.int16),
            pltpu.VMEM((B, R, BS), f32),
            pairs_buf, pairs_buf,
            pltpu.VMEM((R * B, BS), jnp.int16),
            pltpu.VMEM((narrow_count, part, BS), jnp.int16),
            pltpu.VMEM((R * B, BS), f32),
            pltpu.VMEM((part, BS), f32),
            pltpu.VMEM((part, BS), jnp.int16),
            pltpu.VMEM((R * B, BS), jnp.int16),
            pltpu.VMEM((narrow_count, 8, BS), f32),
            pltpu.VMEM((narrow_count, 8, BS), f32),
            pltpu.VMEM((8, BS), f32),
            pltpu.VMEM((narrow_count, 8, BS), f32),
            pltpu.VMEM((2 * R, cols), f32),
            pltpu.VMEM((B, R, BS), f32),
            pltpu.VMEM((R, cols), f32),
            pltpu.VMEM((R, R), f32),
            pltpu.VMEM((2 * R, BS), f32),
            pltpu.VMEM((wide_count, 2 * R, BS), f32),
            wide_sem, wide_sem, wide_sem, wide_sem,
            narrow_sem, narrow_sem, narrow_sem, narrow_sem,
            wide_sem, wide_sem, wide_sem, wide_sem, wide_sem, wide_sem,
            narrow_sem, narrow_sem, narrow_sem, narrow_sem,
        ],
        compiler_params=pltpu.CompilerParams(collective_id=0, has_side_effects=True),
        name="lanczos",
    )(first, local, owners, tiles, q_init)


def per_device(points, q_init, pairs):
    wide_count = lax.axis_size("wide")
    narrow_count = lax.axis_size("narrow")
    me = lax.axis_index("wide")
    own_blocks = points.shape[0] // BS
    width = points.shape[1]
    pair_count = pairs.shape[1]
    capacity = pair_count // wide_count
    total = own_blocks * BS * wide_count
    unit = unit_rows(points).reshape(own_blocks, BS, width)
    turn = jnp.arange(wide_count, dtype=jnp.int32)
    first_rows = (pairs[0] - me * own_blocks).reshape(wide_count, capacity)
    first = first_rows[(me - turn) % wide_count].reshape(pair_count)
    second = (pairs[1].reshape(wide_count, capacity) - turn[:, None] * own_blocks)
    every = lax.all_to_all(
        jnp.broadcast_to(second.reshape(1, pair_count), (wide_count, pair_count)),
        "wide", split_axis=0, concat_axis=0, tiled=True,
    ).reshape(wide_count, wide_count, capacity)
    local_ids = lax.dynamic_index_in_dim(every, me, axis=1, keepdims=False)
    local = local_ids[(me + turn) % wide_count].reshape(pair_count)
    targets = jnp.concatenate([first, local, first, local])
    owners = (jnp.arange(own_blocks, dtype=jnp.int32)[:, None] == targets[None, :]).astype(
        jnp.bfloat16
    )
    buffers = (wide_count - 2) * unit.size * 2
    if wide_count % 2 == 0 and wide_count > 2 and narrow_count == 4 and buffers <= SPREAD_BYTES:
        asked = lax.dynamic_index_in_dim(every, me + 1 - 2 * (me % 2), axis=0, keepdims=False)
        tiles = spread_tiles(
            first, second.reshape(pair_count), asked.reshape(pair_count), unit,
            wide_count, narrow_count,
        )
    else:
        blocks = lax.all_to_all(
            unit[local_ids.reshape(pair_count)], "wide", split_axis=0, concat_axis=0, tiled=True
        ).reshape(wide_count, capacity, BS, width)
        tiles = make_tiles(jnp.reshape(me, (1,)).astype(jnp.int32), first, unit, blocks)
    return lanczos(first, local, owners, tiles, q_init, wide_count, narrow_count, total)


def solution(mesh):
    placed = (P("wide", None), P(None, "wide"), P(None, ("wide", "narrow")))
    return jax.shard_map(
        per_device, mesh=mesh, in_specs=placed, out_specs=(P(None, "wide"), P()), check_vma=False
    )
```
